32 devices in a mesh: groups: 2 (over x), seq: 8 (over z, y), role: 2 (over core).
Axes of the slice: x: 2, y: 2, z: 4, core: 2. Of those that a mesh axis runs over, the one named last changes fastest.
Arguments:
- pair_rep: bfloat16 [512, 256, 128], P(('groups', 'seq', 'role')), parts along dimension 0, may hold values from -6 to 6
- tri_gain: float32 [2, 128], replicated, may hold values from 0.1 to 1.9
- tri_proj: bfloat16 [2, 128, 512], replicated, may hold values from -0.5 to 0.5
- tri_gate: bfloat16 [2, 128, 128], replicated, may hold values from -0.5 to 0.5
- tri_mid_gain: float32 [2, 128], replicated, may hold values from 0.1 to 1.9
- tri_out: bfloat16 [2, 128, 128], replicated, may hold values from -0.5 to 0.5
- trans_gain: float32 [128], replicated, may hold values from 0.1 to 1.9
- trans_up: bfloat16 [128, 1024], replicated, may hold values from -0.5 to 0.5
- trans_down: bfloat16 [512, 128], replicated, may hold values from -0.25 to 0.25
Outputs:
- pair_out: bfloat16 [512, 256, 128], P(('groups', 'seq', 'role')), parts along dimension 0
The draws below stay inside these ranges and needn't reach their ends.
There are 2 independent parts, one for each index of `groups`. The reference program is written for one: setup_inputs(seed, part) draws one part's arguments, and reference() takes and returns one part's arrays. A program takes and returns all parts, laid end to end along the dimension named above; an argument that names none is the same for every part. Nothing has to cross between parts.
All inputs are finite; a program needn't handle non-finite values.
Results may differ from the reference program's by a relative error of at most 0.012.
Values may be sent and summed in bfloat16 or wider, within the bound.
A program may use at most 64 MiB of HBM per device.

```python
import jax
import jax.numpy as jnp
from jax import lax

C = 128
CT = 128
H = 512
TOKENS = 256


def level_of(stream_key, extent, cuts, smallest, high):
    loudness, own = 1.0, jax.random.fold_in(stream_key, 6)
    for axis_at, shards_of in cuts:
        heights = jnp.exp(jax.random.uniform(jax.random.fold_in(own, axis_at), (shards_of,), jnp.float32, smallest / len(cuts), high / len(cuts)))
        loudness = loudness * jnp.repeat(heights, extent[axis_at] // shards_of).reshape([-1 if axis == axis_at else 1 for axis in range(len(extent))])
    return loudness


def noise(own_key, dims, scale, bound, pieces=(), kind=jnp.bfloat16):
    factor_of = level_of(own_key, dims, pieces, -0.22, 0.18) if pieces else 1.0
    entries = jax.random.normal(own_key, dims, jnp.float32) * scale * factor_of
    return jnp.minimum(jnp.maximum(entries, -bound), bound).astype(kind)


def setup_inputs(seed: int = 0, part: int = 0) -> dict:
    keys = jax.random.split(jax.random.key(seed), 10)
    own_keys = jax.random.split(jax.random.fold_in(keys[9], part), 10)
    pair_rep = noise(own_keys[0], (TOKENS, TOKENS, C), 1.0, 6.0, ((0, 16),))
    tri_gain = jnp.clip(1.0 + 0.18 * jax.random.normal(keys[1], (2, C), jnp.float32), 0.1, 1.9)
    tri_proj = noise(keys[2], (2, C, 4 * CT), C ** -0.5, 0.5)
    tri_gate = noise(keys[3], (2, C, C), C ** -0.5, 0.5)
    tri_mid_gain = jnp.clip(1.0 + 0.18 * jax.random.normal(keys[4], (2, CT), jnp.float32), 0.1, 1.9)
    tri_out = noise(keys[5], (2, CT, C), CT ** -0.5, 0.5)
    trans_gain = jnp.clip(1.0 + 0.18 * jax.random.normal(keys[6], (C,), jnp.float32), 0.1, 1.9)
    trans_up = noise(keys[7], (C, 2 * H), C ** -0.5, 0.5)
    trans_down = noise(keys[8], (H, C), H ** -0.5, 0.25)
    return dict(pair_rep=pair_rep, tri_gain=tri_gain, tri_proj=tri_proj, tri_gate=tri_gate, tri_mid_gain=tri_mid_gain, tri_out=tri_out, trans_gain=trans_gain, trans_up=trans_up, trans_down=trans_down)


epsilon = 1e-05

def layer_norm(values, gain):
    average = lax.optimization_barrier(jnp.mean(values, axis=-1, keepdims=True))
    centred = values - average
    spread = lax.optimization_barrier(jnp.mean(centred * centred, axis=-1, keepdims=True))
    return centred * lax.rsqrt(spread + epsilon) * gain

def reference(pair_rep, tri_gain, tri_proj, tri_gate, tri_mid_gain, tri_out, trans_gain, trans_up, trans_down):
    tokens_all = pair_rep.shape[0]
    channels = pair_rep.shape[2]
    inner = tri_out.shape[1]
    hidden_width = trans_down.shape[0]
    block_rows = 16
    block_count = tokens_all // block_rows
    current = pair_rep
    for which in range(2):

        def project(block_in):
            normed = layer_norm(block_in.astype(jnp.float32), tri_gain[which]).astype(jnp.bfloat16)
            projected = jnp.dot(normed, tri_proj[which], preferred_element_type=jnp.float32)
            left_side = (projected[..., :inner] * jax.nn.sigmoid(projected[..., inner:2 * inner])).astype(jnp.bfloat16)
            right_side = (projected[..., 2 * inner:3 * inner] * jax.nn.sigmoid(projected[..., 3 * inner:])).astype(jnp.bfloat16)
            gating = jax.nn.sigmoid(jnp.dot(normed, tri_gate[which], preferred_element_type=jnp.float32))
            return (left_side, right_side, gating)
        left_side, right_side, gating = lax.map(project, current.reshape(block_count, block_rows, tokens_all, channels))
        left_side = left_side.reshape(tokens_all, tokens_all, inner).astype(jnp.float32)
        right_side = right_side.reshape(tokens_all, tokens_all, inner).astype(jnp.float32)
        gating = gating.reshape(tokens_all, tokens_all, channels)
        if which == 0:
            product = jnp.einsum('ikc,jkc->ijc', left_side, right_side)
        else:
            product = jnp.einsum('kic,kjc->ijc', left_side, right_side)
        product = product.astype(jnp.bfloat16)
        normed_mid = layer_norm(product.astype(jnp.float32), tri_mid_gain[which]).astype(jnp.bfloat16)
        update = jnp.dot(normed_mid, tri_out[which], preferred_element_type=jnp.float32)
        current = (current.astype(jnp.float32) + gating * update).astype(jnp.bfloat16)

    def transition(block_in):
        normed = layer_norm(block_in.astype(jnp.float32), trans_gain).astype(jnp.bfloat16)
        values = jnp.dot(normed, trans_up, preferred_element_type=jnp.float32)
        hidden = (jax.nn.silu(values[..., :hidden_width]) * values[..., hidden_width:]).astype(jnp.bfloat16)
        down = jnp.dot(hidden, trans_down, preferred_element_type=jnp.float32)
        return (block_in.astype(jnp.float32) + down).astype(jnp.bfloat16)
    result = lax.map(transition, current.reshape(block_count, block_rows, tokens_all, channels))
    return result.reshape(tokens_all, tokens_all, channels)
```

```python
import functools

import jax
import jax.numpy as jnp
from jax import lax
from jax.experimental import pallas as pl
from jax.experimental.pallas import tpu as pltpu
from jax.sharding import PartitionSpec as P

epsilon = 1e-05
MESH = pl.DeviceIdType.MESH
LANES = 128
CB = 16


def sigmoid(v):
    return 0.5 * jnp.tanh(0.5 * v) + 0.5


def norm(v, gain, axis):
    average = jnp.mean(v, axis=axis, keepdims=True)
    centred = v - average
    spread = jnp.mean(centred * centred, axis=axis, keepdims=True)
    return (centred * lax.rsqrt(spread + epsilon) * gain).astype(jnp.bfloat16)


def dot(a, b, da, db):
    return lax.dot_general(a, b, (((da,), (db,)), ((), ())), preferred_element_type=jnp.float32)


def kernel(
    N, M, Q, R, roles,
    pair, gain, projT, gatew, midg, outw, tgain, up, down, out,
    lbuf, rbuf, cur1, gates, l0, r0, l1, r1, lT, rT, pT, psend, precv, xsend, xrecv, own,
    ls, lr, rs, rr, l1s, l1r, r1s, r1r, ps, pr, xs, xr,
):
    C = pair.shape[2]
    inner = outw.shape[1]
    hidden = down.shape[0]
    me = lax.axis_index("seq") * roles + lax.axis_index("role")
    q, m = lax.div(me, M), lax.rem(me, M)
    part = M * R

    def where(d):
        return {"seq": lax.div(d, roles), "role": lax.rem(d, roles)}

    def loop(count, body, unroll=1):
        def step(i, carry):
            body(i)
            return carry
        lax.fori_loop(0, count, step, 0, unroll=unroll)

    def lanes(p):
        return pl.ds(pl.multiple_of(p * LANES, LANES), LANES)

    def chans(u):
        return pl.ds(pl.multiple_of(u * CB, CB), CB)

    def rows(u, size):
        return pl.ds(pl.multiple_of(u * size, size), size)

    def remote(src, dst, ssem, rsem, d):
        return pltpu.make_async_remote_copy(
            src_ref=src, dst_ref=dst, send_sem=ssem, recv_sem=rsem,
            device_id=where(d), device_id_type=MESH)

    barrier = pltpu.get_barrier_semaphore()
    def greet(i):
        pl.semaphore_signal(barrier, inc=1, device_id=where(lax.rem(me + 1 + i, N)), device_id_type=MESH)
    loop(N - 1, greet)

    def project(t, cur, p):
        def row(r):
            x = cur[r, lanes(p), :].astype(jnp.float32)
            xn = norm(x, gain[t : t + 1, :], 1)
            pj = dot(projT[t], xn, 1, 1)
            lbuf[t, r, :, lanes(p)] = (pj[:inner] * sigmoid(pj[inner : 2 * inner])).astype(jnp.bfloat16)
            rbuf[t, r, :, lanes(p)] = (pj[2 * inner : 3 * inner] * sigmoid(pj[3 * inner :])).astype(jnp.bfloat16)
            gates[r, lanes(p), :] = sigmoid(dot(xn, gatew[t], 1, 0))
        loop(R, row, 2)

    def left_copy(t, u, p, src):
        dst, s, r_ = (l0, ls, lr) if t == 0 else (l1, l1s, l1r)
        return remote(lbuf.at[t, :, chans(u), lanes(p)], dst.at[rows(src, R), :, lanes(p)],
                      s.at[u, p], r_.at[src, p], q * M + u)

    def right_copy(t, d, p, src):
        if t == 0:
            return remote(rbuf.at[t, :, chans(lax.rem(d, M)), lanes(p)], r0.at[rows(src, R), :, lanes(p)],
                          rs.at[d, p], rr.at[src, p], d)
        return remote(rbuf.at[t, :, chans(d), lanes(p)], r1.at[rows(src, R), :, lanes(p)],
                      r1s.at[d, p], r1r.at[src, p], q * M + d)

    def self_copies(t, p):
        dl, sl = (l0, lr) if t == 0 else (l1, l1r)
        dr, sr, at = (r0, rr, me) if t == 0 else (r1, r1r, m)
        return (pltpu.make_async_copy(lbuf.at[t, :, chans(m), lanes(p)], dl.at[rows(m, R), :, lanes(p)], sl.at[m, p]),
                pltpu.make_async_copy(rbuf.at[t, :, chans(m), lanes(p)], dr.at[rows(at, R), :, lanes(p)], sr.at[at, p]))

    def send_lr(t, p):
        for c in self_copies(t, p):
            c.start()
        def near(i):
            u = lax.rem(m + 1 + i, M)
            left_copy(t, u, p, m).start()
            right_copy(t, q * M + u if t == 0 else u, p, me if t == 0 else m).start()
        if t == 0:
            def far(i):
                d = lax.rem(q + 1 + lax.div(i, M), Q) * M + lax.rem(m + i, M)
                right_copy(0, d, p, me).start()
            loop(N - M, far)
        loop(M - 1, near)

    def swap(x):
        return jnp.swapaxes(x, 0, 1)

    def back_copy(t, u, p, src):
        return remote(psend.at[t, p, u], precv.at[t, :, chans(src), lanes(p)],
                      ps.at[t, u, p], pr.at[t, src, p], q * M + u)

    def send_back(t, p):
        def one(u):
            psend[t, p, u] = swap(pT[:, rows(u, R), :])
        loop(M, one)
        pltpu.make_async_copy(psend.at[t, p, m], precv.at[t, :, chans(m), lanes(p)], pr.at[t, m, p]).start()
        def go(i):
            back_copy(t, lax.rem(m + 1 + i, M), p, m).start()
        loop(M - 1, go)

    def wait_back(t, p):
        def one(u):
            pltpu.make_async_copy(psend.at[t, p, u], precv.at[t, :, chans(u), lanes(p)], pr.at[t, u, p]).wait()
        loop(M, one)

    def updated(t, cur, r, p):
        y = precv[t, r, :, lanes(p)].astype(jnp.float32)
        yn = norm(y, midg[t], 0)
        upd = dot(yn, outw[t], 0, 0)
        return (cur[r, lanes(p), :].astype(jnp.float32) + gates[r, lanes(p), :] * upd).astype(jnp.bfloat16)

    for s in range(Q):
        project(0, pair, s)
        if s == 0:
            pl.semaphore_wait(barrier, N - 1)
        send_lr(0, s)
    for s in range(Q):
        p = lax.rem(q + s, Q)
        def arrive(u, s=s, p=p):
            at = p * M + u
            for h in range(Q):
                pltpu.make_async_copy(rbuf.at[0, :, chans(u), lanes(h)], r0.at[rows(at, R), :, lanes(h)], rr.at[at, h]).wait()
                if s == 0:
                    pltpu.make_async_copy(lbuf.at[0, :, chans(u), lanes(h)], l0.at[rows(u, R), :, lanes(h)], lr.at[u, h]).wait()
            rT[:, rows(u, R), :] = swap(r0[rows(at, R)])
            if s == 0:
                lT[:, rows(u, R), :] = swap(l0[rows(u, R)])
        loop(M, arrive)
        def product(c):
            pT[c] = dot(lT[c], rT[c], 1, 1).astype(jnp.bfloat16)
        loop(CB, product, 2)
        send_back(0, p)
    for s in range(Q):
        p = lax.rem(q + s, Q)
        wait_back(0, p)
        def row(r, p=p):
            cur1[r, lanes(p), :] = updated(0, pair, r, p)
        loop(R, row, 2)
        project(1, cur1, p)
        send_lr(1, p)
    def arrive1(u):
        for h in range(Q):
            pltpu.make_async_copy(rbuf.at[1, :, chans(u), lanes(h)], r1.at[rows(u, R), :, lanes(h)], r1r.at[u, h]).wait()
            pltpu.make_async_copy(lbuf.at[1, :, chans(u), lanes(h)], l1.at[rows(u, R), :, lanes(h)], l1r.at[u, h]).wait()
        rT[:, rows(u, R), :] = swap(r1[rows(u, R)])
        lT[:, rows(u, R), :] = swap(l1[rows(u, R)])
    loop(M, arrive1)

    def cross(d, p):
        return remote(xsend.at[d - 1, p], xrecv.at[d - 1, p], xs.at[d - 1, p], xr.at[d - 1, p],
                      lax.rem(q + d, Q) * M + m)

    for p in range(Q):
        for d in range(1, Q):
            other = lax.rem(q + d, Q)
            def partial(c, d=d, p=p, other=other):
                xsend[d - 1, p, c] = dot(lT[c, :, lanes(other)], rT[c, :, lanes(p)], 0, 0).astype(jnp.bfloat16)
            loop(CB, partial, 2)
            cross(d, p).start()
    for p in range(Q):
        def mine(c, p=p):
            own[p, c] = dot(lT[c, :, lanes(q)], rT[c, :, lanes(p)], 0, 0)
        loop(CB, mine, 2)
    for p in range(Q):
        for d in range(1, Q):
            cross(d, p).wait_recv()
        def total(c, p=p):
            v = own[p, c]
            for d in range(1, Q):
                v = v + xrecv[d - 1, p, c].astype(jnp.float32)
            pT[c] = v.astype(jnp.bfloat16)
        loop(CB, total, 2)
        send_back(1, p)
    for p in range(Q):
        wait_back(1, p)
        def last(r, p=p):
            cur = updated(1, cur1, r, p).astype(jnp.float32)
            xn = norm(cur, tgain[...], 1)
            val = dot(xn, up[...], 1, 0)
            q0, q1 = val[:, :hidden], val[:, hidden:]
            h = (q0 * sigmoid(q0) * q1).astype(jnp.bfloat16)
            out[r, lanes(p), :] = (cur + dot(h, down[...], 1, 0)).astype(jnp.bfloat16)
        loop(R, last, 2)
    def drain(i):
        u = lax.rem(m + 1 + i, M)
        for p in range(Q):
            left_copy(0, u, p, m).wait_send()
            left_copy(1, u, p, m).wait_send()
            right_copy(1, u, p, m).wait_send()
            for t in range(2):
                back_copy(t, u, p, m).wait_send()
    loop(M - 1, drain)
    def drain_right(i):
        d = lax.rem(me + 1 + i, N)
        for p in range(Q):
            right_copy(0, d, p, me).wait_send()
    loop(N - 1, drain_right)
    for p in range(Q):
        for d in range(1, Q):
            cross(d, p).wait_send()


def solution(mesh):
    N = mesh.shape["seq"] * mesh.shape["role"]
    roles = mesh.shape["role"]

    def local(pair, tri_gain, tri_proj, tri_gate, tri_mid_gain, tri_out, trans_gain, trans_up, trans_down):
        R, W, C = pair.shape
        inner = tri_out.shape[1]
        M = inner // CB
        Q = N // M
        bf, f32, vm, dma = jnp.bfloat16, jnp.float32, pltpu.VMEM, pltpu.SemaphoreType.DMA
        part = M * R
        assert part == LANES and Q * LANES == W
        X = max(Q - 1, 1)
        return pl.pallas_call(
            functools.partial(kernel, N, M, Q, R, roles),
            out_shape=jax.ShapeDtypeStruct((R, W, C), bf),
            in_specs=[pl.BlockSpec(memory_space=vm)] * 9,
            out_specs=pl.BlockSpec(memory_space=vm),
            scratch_shapes=[
                vm((2, R, inner, W), bf), vm((2, R, inner, W), bf),
                vm((R, W, C), bf), vm((R, W, C), f32),
                vm((part, CB, W), bf), vm((W, CB, W), bf),
                vm((part, CB, W), bf), vm((part, CB, W), bf),
                vm((CB, part, W), bf), vm((CB, part, W), bf), vm((CB, part, LANES), bf),
                vm((2, Q, M, R, CB, LANES), bf), vm((2, R, inner, W), bf),
                vm((X, Q, CB, part, LANES), bf), vm((X, Q, CB, part, LANES), bf),
                vm((Q, CB, part, LANES), f32),
                dma((M, Q)), dma((M, Q)), dma((N, Q)), dma((N, Q)),
                dma((M, Q)), dma((M, Q)), dma((M, Q)), dma((M, Q)),
                dma((2, M, Q)), dma((2, M, Q)), dma((X, Q)), dma((X, Q)),
            ],
            compiler_params=pltpu.CompilerParams(
                collective_id=0, has_side_effects=True, vmem_limit_bytes=66_000_000),
        )(pair, tri_gain, jnp.swapaxes(tri_proj, 1, 2), tri_gate, tri_mid_gain[:, :, None], tri_out,
          trans_gain[None, :], trans_up, trans_down)

    in_specs = (P(("groups", "seq", "role"), None, None), P(), P(), P(), P(), P(), P(), P(), P())
    out_specs = P(("groups", "seq", "role"), None, None)
    return jax.shard_map(local, mesh=mesh, in_specs=in_specs, out_specs=out_specs, check_vma=False)
```

```python
import functools

import jax
import jax.numpy as jnp
from jax import lax
from jax.experimental import pallas as pl
from jax.experimental.pallas import tpu as pltpu
from jax.sharding import PartitionSpec as P

epsilon = 1e-05
MESH = pl.DeviceIdType.MESH
LANES = 128
G = 4
CB = 16


def sigmoid(v):
    return 0.5 * jnp.tanh(0.5 * v) + 0.5


def norm(v, gain, axis):
    average = jnp.mean(v, axis=axis, keepdims=True)
    centred = v - average
    spread = jnp.mean(centred * centred, axis=axis, keepdims=True)
    return (centred * lax.rsqrt(spread + epsilon) * gain).astype(jnp.bfloat16)


def dot(a, b, da, db):
    return lax.dot_general(a, b, (((da,), (db,)), ((), ())), preferred_element_type=jnp.float32)


def kernel(
    N, M, Q, R, roles,
    pair, gain, projT, gatew, midg, outw, tgain, up, down, out,
    lbuf, rbuf, cur1, gates, l0, r0, l1, r1, lT, rT, pT, psend, precv, xsend, xrecv, own,
    ls, lr, rs, rr, l1s, l1r, r1s, r1r, ps, pr, xs, xr,
):
    C = pair.shape[2]
    inner = outw.shape[1]
    hidden = down.shape[0]
    me = lax.axis_index("seq") * roles + lax.axis_index("role")
    q, m = lax.div(me, M), lax.rem(me, M)
    part = M * R

    def where(d):
        return {"seq": lax.div(d, roles), "role": lax.rem(d, roles)}

    def loop(count, body, unroll=1):
        def step(i, carry):
            body(i)
            return carry
        lax.fori_loop(0, count, step, 0, unroll=unroll)

    def lanes(p):
        return pl.ds(pl.multiple_of(p * LANES, LANES), LANES)

    def chans(u):
        return pl.ds(pl.multiple_of(u * CB, CB), CB)

    def rows(u, size):
        return pl.ds(pl.multiple_of(u * size, size), size)

    def remote(src, dst, ssem, rsem, d):
        return pltpu.make_async_remote_copy(
            src_ref=src, dst_ref=dst, send_sem=ssem, recv_sem=rsem,
            device_id=where(d), device_id_type=MESH)

    barrier = pltpu.get_barrier_semaphore()
    def greet(i):
        pl.semaphore_signal(barrier, inc=1, device_id=where(lax.rem(me + 1 + i, N)), device_id_type=MESH)
    loop(N - 1, greet)

    def tokens(cur, r, p):
        return cur[pl.ds(r * G, G), lanes(p), :].astype(jnp.float32).reshape(G * LANES, C)

    def project(t, cur, p):
        def row(r):
            xn = norm(tokens(cur, r, p), gain[t : t + 1, :], 1)
            gates[pl.ds(r * G, G), lanes(p), :] = sigmoid(dot(xn, gatew[t], 1, 0)).reshape(G, LANES, C)
            for buf, at in ((lbuf, 0), (rbuf, 2 * inner)):
                pj = dot(projT[t, at : at + 2 * inner], xn, 1, 1)
                v = (pj[:inner] * sigmoid(pj[inner:])).astype(jnp.bfloat16)
                for g in range(G):
                    buf[t, r * G + g, :, lanes(p)] = v[:, g * LANES : (g + 1) * LANES]
        loop(R // G, row)

    def left_copy(t, u, p, src):
        dst, s, r_ = (l0, ls, lr) if t == 0 else (l1, l1s, l1r)
        return remote(lbuf.at[t, :, chans(u), lanes(p)], dst.at[rows(src, R), :, lanes(p)],
                      s.at[u, p], r_.at[src, p], q * M + u)

    def right_copy(t, d, p, src):
        if t == 0:
            return remote(rbuf.at[t, :, chans(lax.rem(d, M)), lanes(p)], r0.at[rows(src, R), :, lanes(p)],
                          rs.at[d, p], rr.at[src, p], d)
        return remote(rbuf.at[t, :, chans(d), lanes(p)], r1.at[rows(src, R), :, lanes(p)],
                      r1s.at[d, p], r1r.at[src, p], q * M + d)

    def self_copies(t, p):
        dl, sl = (l0, lr) if t == 0 else (l1, l1r)
        dr, sr, at = (r0, rr, me) if t == 0 else (r1, r1r, m)
        return (pltpu.make_async_copy(lbuf.at[t, :, chans(m), lanes(p)], dl.at[rows(m, R), :, lanes(p)], sl.at[m, p]),
                pltpu.make_async_copy(rbuf.at[t, :, chans(m), lanes(p)], dr.at[rows(at, R), :, lanes(p)], sr.at[at, p]))

    def send_lr(t, p):
        for c in self_copies(t, p):
            c.start()
        def near_left(i):
            left_copy(t, lax.rem(m + 1 + i, M), p, m).start()
        def near_right(i):
            u = lax.rem(m + 1 + i, M)
            right_copy(t, q * M + u if t == 0 else u, p, me if t == 0 else m).start()
        loop(M - 1, near_left)
        loop(M - 1, near_right)

    def send_far(p):
        def far(i):
            d = lax.rem(q + 1 + lax.div(i, M), Q) * M + lax.rem(m + i, M)
            right_copy(0, d, p, me).start()
        loop(N - M, far)

    def swap(x):
        return jnp.swapaxes(x, 0, 1)

    def back_copy(t, u, p, src):
        return remote(psend.at[t, p, u], precv.at[t, :, chans(src), lanes(p)],
                      ps.at[t, u, p], pr.at[t, src, p], q * M + u)

    def send_back(t, p):
        def one(u):
            psend[t, p, u] = swap(pT[:, rows(u, R), :])
        loop(M, one)
        pltpu.make_async_copy(psend.at[t, p, m], precv.at[t, :, chans(m), lanes(p)], pr.at[t, m, p]).start()
        def go(i):
            back_copy(t, lax.rem(m + 1 + i, M), p, m).start()
        loop(M - 1, go)

    def wait_back(t, p):
        def one(u):
            pltpu.make_async_copy(psend.at[t, p, u], precv.at[t, :, chans(u), lanes(p)], pr.at[t, u, p]).wait()
        loop(M, one)

    def updated(t, cur, r, p, to):
        for g in range(G):
            y = precv[t, r * G + g, :, lanes(p)].astype(jnp.float32)
            yn = norm(y, midg[t], 0)
            upd = dot(yn, outw[t], 0, 0)
            to[r * G + g, lanes(p), :] = (cur[r * G + g, lanes(p), :].astype(jnp.float32)
                                          + gates[r * G + g, lanes(p), :] * upd).astype(jnp.bfloat16)

    def finish(p):
        wait_back(1, p)
        def last(r):
            updated(1, cur1, r, p, cur1)
            cur = tokens(cur1, r, p)
            xn = norm(cur, tgain[...], 1)
            val = dot(xn, up[...], 1, 0)
            q0, q1 = val[:, :hidden], val[:, hidden:]
            h = (q0 * sigmoid(q0) * q1).astype(jnp.bfloat16)
            out[pl.ds(r * G, G), lanes(p), :] = (cur + dot(h, down[...], 1, 0)).astype(jnp.bfloat16).reshape(G, LANES, C)
        loop(R // G, last)

    for s in range(Q):
        project(0, pair, s)
        if s == 0:
            pl.semaphore_wait(barrier, N - 1)
        send_lr(0, s)
        send_far(s)
    for s in range(Q):
        p = lax.rem(q + s, Q)
        def arrive(u, s=s, p=p):
            at = p * M + u
            for h in range(Q):
                pltpu.make_async_copy(rbuf.at[0, :, chans(u), lanes(h)], r0.at[rows(at, R), :, lanes(h)], rr.at[at, h]).wait()
                if s == 0:
                    pltpu.make_async_copy(lbuf.at[0, :, chans(u), lanes(h)], l0.at[rows(u, R), :, lanes(h)], lr.at[u, h]).wait()
            rT[:, rows(u, R), :] = swap(r0[rows(at, R)])
            if s == 0:
                lT[:, rows(u, R), :] = swap(l0[rows(u, R)])
        loop(M, arrive)
        def product(c):
            pT[c] = dot(lT[c], rT[c], 1, 1).astype(jnp.bfloat16)
        loop(CB, product, 4)
        send_back(0, p)
        wait_back(0, p)
        def row(r, p=p):
            updated(0, pair, r, p, cur1)
        loop(R // G, row)
        project(1, cur1, p)
        send_lr(1, p)

    def left_here(p):
        def one(u):
            pltpu.make_async_copy(lbuf.at[1, :, chans(u), lanes(p)], l1.at[rows(u, R), :, lanes(p)], l1r.at[u, p]).wait()
            lT[:, rows(u, R), lanes(p)] = swap(l1[rows(u, R), :, lanes(p)])
        loop(M, one)

    def right_here(p):
        def one(u):
            pltpu.make_async_copy(rbuf.at[1, :, chans(u), lanes(p)], r1.at[rows(u, R), :, lanes(p)], r1r.at[u, p]).wait()
            rT[:, rows(u, R), lanes(p)] = swap(r1[rows(u, R), :, lanes(p)])
        loop(M, one)

    def cross(d, p):
        return remote(xsend.at[d - 1, p], xrecv.at[d - 1, p], xs.at[d - 1, p], xr.at[d - 1, p],
                      lax.rem(q + d, Q) * M + m)

    left_here(q)
    for s in range(Q):
        p = lax.rem(q + s, Q)
        right_here(p)
        for d in range(1, Q):
            other = lax.rem(q + d, Q)
            if s == 0:
                left_here(other)
            def partial(c, d=d, p=p, other=other):
                xsend[d - 1, p, c] = dot(lT[c, :, lanes(other)], rT[c, :, lanes(p)], 0, 0).astype(jnp.bfloat16)
            loop(CB, partial, 4)
            cross(d, p).start()
    for p in range(Q):
        def mine(c, p=p):
            own[p, c] = dot(lT[c, :, lanes(q)], rT[c, :, lanes(p)], 0, 0)
        loop(CB, mine, 4)
    for s in range(Q):
        p = lax.rem(q + 1 + s, Q)
        for d in range(1, Q):
            cross(d, p).wait_recv()
        def total(c, p=p):
            v = own[p, c]
            for d in range(1, Q):
                v = v + xrecv[d - 1, p, c].astype(jnp.float32)
            pT[c] = v.astype(jnp.bfloat16)
        loop(CB, total, 2)
        send_back(1, p)
        if s > 0:
            finish(lax.rem(q + s, Q))
    finish(lax.rem(q + Q, Q))
    def drain(i):
        u = lax.rem(m + 1 + i, M)
        for p in range(Q):
            left_copy(0, u, p, m).wait_send()
            left_copy(1, u, p, m).wait_send()
            right_copy(1, u, p, m).wait_send()
            for t in range(2):
                back_copy(t, u, p, m).wait_send()
    loop(M - 1, drain)
    def drain_right(i):
        d = lax.rem(me + 1 + i, N)
        for p in range(Q):
            right_copy(0, d, p, me).wait_send()
    loop(N - 1, drain_right)
    for p in range(Q):
        for d in range(1, Q):
            cross(d, p).wait_send()


def solution(mesh):
    N = mesh.shape["seq"] * mesh.shape["role"]
    roles = mesh.shape["role"]

    def local(pair, tri_gain, tri_proj, tri_gate, tri_mid_gain, tri_out, trans_gain, trans_up, trans_down):
        R, W, C = pair.shape
        inner = tri_out.shape[1]
        M = inner // CB
        Q = N // M
        bf, f32, vm, dma = jnp.bfloat16, jnp.float32, pltpu.VMEM, pltpu.SemaphoreType.DMA
        part = M * R
        assert part == LANES and Q * LANES == W
        X = max(Q - 1, 1)
        return pl.pallas_call(
            functools.partial(kernel, N, M, Q, R, roles),
            out_shape=jax.ShapeDtypeStruct((R, W, C), bf),
            in_specs=[pl.BlockSpec(memory_space=vm)] * 9,
            out_specs=pl.BlockSpec(memory_space=vm),
            scratch_shapes=[
                vm((2, R, inner, W), bf), vm((2, R, inner, W), bf),
                vm((R, W, C), bf), vm((R, W, C), f32),
                vm((part, CB, W), bf), vm((W, CB, W), bf),
                vm((part, CB, W), bf), vm((part, CB, W), bf),
                vm((CB, part, W), bf), vm((CB, part, W), bf), vm((CB, part, LANES), bf),
                vm((2, Q, M, R, CB, LANES), bf), vm((2, R, inner, W), bf),
                vm((X, Q, CB, part, LANES), bf), vm((X, Q, CB, part, LANES), bf),
                vm((Q, CB, part, LANES), f32),
                dma((M, Q)), dma((M, Q)), dma((N, Q)), dma((N, Q)),
                dma((M, Q)), dma((M, Q)), dma((M, Q)), dma((M, Q)),
                dma((2, M, Q)), dma((2, M, Q)), dma((X, Q)), dma((X, Q)),
            ],
            compiler_params=pltpu.CompilerParams(
                collective_id=0, has_side_effects=True, vmem_limit_bytes=66_000_000),
        )(pair, tri_gain, jnp.swapaxes(tri_proj, 1, 2), tri_gate, tri_mid_gain[:, :, None], tri_out,
          trans_gain[None, :], trans_up, trans_down)

    in_specs = (P(("groups", "seq", "role"), None, None), P(), P(), P(), P(), P(), P(), P(), P())
    out_specs = P(("groups", "seq", "role"), None, None)
    return jax.shard_map(local, mesh=mesh, in_specs=in_specs, out_specs=out_specs, check_vma=False)
```

```python
import functools

import jax
import jax.numpy as jnp
from jax import lax
from jax.experimental import pallas as pl
from jax.experimental.pallas import tpu as pltpu
from jax.sharding import PartitionSpec as P

epsilon = 1e-05
MESH = pl.DeviceIdType.MESH
LANES = 128
G = 4
KS = 2
CB = 16
KB = CB // KS


def sigmoid(v):
    return 0.5 * jnp.tanh(0.5 * v) + 0.5


def norm(v, gain, axis):
    average = jnp.mean(v, axis=axis, keepdims=True)
    centred = v - average
    spread = jnp.mean(centred * centred, axis=axis, keepdims=True)
    return (centred * lax.rsqrt(spread + epsilon) * gain).astype(jnp.bfloat16)


def dot(a, b, da, db):
    return lax.dot_general(a, b, (((da,), (db,)), ((), ())), preferred_element_type=jnp.float32)


def kernel(
    N, M, Q, R, roles,
    pair, gain, projT, gatew, midg, outw, tgain, up, down, out,
    lbuf, rbuf, cur1, gates, l0, r0, l1, r1, lT, rT, pT, psend, precv, xsend, xrecv, own,
    ls, lr, rs, rr, l1s, l1r, r1s, r1r, ps, pr, xs, xr,
):
    C = pair.shape[2]
    inner = outw.shape[1]
    hidden = down.shape[0]
    me = lax.axis_index("seq") * roles + lax.axis_index("role")
    q, m = lax.div(me, M), lax.rem(me, M)
    part = M * R

    def where(d):
        return {"seq": lax.div(d, roles), "role": lax.rem(d, roles)}

    def loop(count, body, unroll=1):
        def step(i, carry):
            body(i)
            return carry
        lax.fori_loop(0, count, step, 0, unroll=unroll)

    def lanes(p):
        return pl.ds(pl.multiple_of(p * LANES, LANES), LANES)

    def chans(u):
        return pl.ds(pl.multiple_of(u * CB, CB), CB)

    def rows(u, size):
        return pl.ds(pl.multiple_of(u * size, size), size)

    def remote(src, dst, ssem, rsem, d):
        return pltpu.make_async_remote_copy(
            src_ref=src, dst_ref=dst, send_sem=ssem, recv_sem=rsem,
            device_id=where(d), device_id_type=MESH)

    barrier = pltpu.get_barrier_semaphore()
    def greet(i):
        pl.semaphore_signal(barrier, inc=1, device_id=where(lax.rem(me + 1 + i, N)), device_id_type=MESH)
    loop(N - 1, greet)

    def tokens(cur, r, p):
        return cur[pl.ds(r * G, G), lanes(p), :].astype(jnp.float32).reshape(G * LANES, C)

    def project(t, cur, p):
        def row(r):
            xn = norm(tokens(cur, r, p), gain[t : t + 1, :], 1)
            gates[pl.ds(r * G, G), lanes(p), :] = sigmoid(dot(xn, gatew[t], 1, 0)).reshape(G, LANES, C)
            for buf, at in ((lbuf, 0), (rbuf, 2 * inner)):
                pj = dot(projT[t, at : at + 2 * inner], xn, 1, 1)
                v = (pj[:inner] * sigmoid(pj[inner:])).astype(jnp.bfloat16)
                for g in range(G):
                    buf[t, r * G + g, :, lanes(p)] = v[:, g * LANES : (g + 1) * LANES]
        loop(R // G, row)

    def left_copy(t, u, p, src):
        dst, s, r_ = (l0, ls, lr) if t == 0 else (l1, l1s, l1r)
        return remote(lbuf.at[t, :, chans(u), lanes(p)], dst.at[rows(src, R), :, lanes(p)],
                      s.at[u, p], r_.at[src, p], q * M + u)

    def right_copy(t, d, p, src):
        if t == 0:
            return remote(rbuf.at[t, :, chans(lax.rem(d, M)), lanes(p)], r0.at[rows(src, R), :, lanes(p)],
                          rs.at[d, p], rr.at[src, p], d)
        return remote(rbuf.at[t, :, chans(d), lanes(p)], r1.at[rows(src, R), :, lanes(p)],
                      r1s.at[d, p], r1r.at[src, p], q * M + d)

    def self_copy(side, t, p):
        dl, sl = (l0, lr) if t == 0 else (l1, l1r)
        dr, sr, at = (r0, rr, me) if t == 0 else (r1, r1r, m)
        if side == 0:
            return pltpu.make_async_copy(lbuf.at[t, :, chans(m), lanes(p)], dl.at[rows(m, R), :, lanes(p)], sl.at[m, p])
        return pltpu.make_async_copy(rbuf.at[t, :, chans(m), lanes(p)], dr.at[rows(at, R), :, lanes(p)], sr.at[at, p])

    def send_left(t, p):
        self_copy(0, t, p).start()
        def near(i):
            left_copy(t, lax.rem(m + 1 + i, M), p, m).start()
        loop(M - 1, near)

    def send_right(t, p):
        self_copy(1, t, p).start()
        def near(i):
            u = lax.rem(m + 1 + i, M)
            right_copy(t, q * M + u if t == 0 else u, p, me if t == 0 else m).start()
        loop(M - 1, near)

    def send_far(p):
        def far(i):
            d = lax.rem(q + 1 + lax.div(i, M), Q) * M + lax.rem(m + i, M)
            right_copy(0, d, p, me).start()
        loop(N - M, far)

    def swap(x):
        return jnp.swapaxes(x, 0, 1)

    def back_copy(t, u, p, src):
        return remote(psend.at[t, p, u], precv.at[t, :, chans(src), lanes(p)],
                      ps.at[t, u, p], pr.at[t, src, p], q * M + u)

    def send_back(t, p):
        def one(u):
            psend[t, p, u] = swap(pT[:, rows(u, R), :])
        loop(M, one)
        pltpu.make_async_copy(psend.at[t, p, m], precv.at[t, :, chans(m), lanes(p)], pr.at[t, m, p]).start()
        def go(i):
            back_copy(t, lax.rem(m + 1 + i, M), p, m).start()
        loop(M - 1, go)

    def wait_back(t, p):
        def one(u):
            pltpu.make_async_copy(psend.at[t, p, u], precv.at[t, :, chans(u), lanes(p)], pr.at[t, u, p]).wait()
        loop(M, one)

    def updated(t, cur, r, p, to):
        for g in range(G):
            y = precv[t, r * G + g, :, lanes(p)].astype(jnp.float32)
            yn = norm(y, midg[t], 0)
            upd = dot(yn, outw[t], 0, 0)
            to[r * G + g, lanes(p), :] = (cur[r * G + g, lanes(p), :].astype(jnp.float32)
                                          + gates[r * G + g, lanes(p), :] * upd).astype(jnp.bfloat16)

    def finish(p):
        wait_back(1, p)
        def last(r):
            updated(1, cur1, r, p, cur1)
            cur = tokens(cur1, r, p)
            xn = norm(cur, tgain[...], 1)
            val = dot(xn, up[...], 1, 0)
            q0, q1 = val[:, :hidden], val[:, hidden:]
            h = (q0 * sigmoid(q0) * q1).astype(jnp.bfloat16)
            out[pl.ds(r * G, G), lanes(p), :] = (cur + dot(h, down[...], 1, 0)).astype(jnp.bfloat16).reshape(G, LANES, C)
        loop(R // G, last)

    for s in range(Q):
        project(0, pair, s)
        if s == 0:
            pl.semaphore_wait(barrier, N - 1)
        send_left(0, s)
        send_right(0, s)
    for s in range(Q):
        send_far(s)
    for s in range(Q):
        p = lax.rem(q + s, Q)
        def arrive(u, s=s, p=p):
            at = p * M + u
            for h in range(Q):
                pltpu.make_async_copy(rbuf.at[0, :, chans(u), lanes(h)], r0.at[rows(at, R), :, lanes(h)], rr.at[at, h]).wait()
                if s == 0:
                    pltpu.make_async_copy(lbuf.at[0, :, chans(u), lanes(h)], l0.at[rows(u, R), :, lanes(h)], lr.at[u, h]).wait()
            rT[:, rows(u, R), :] = swap(r0[rows(at, R)])
            if s == 0:
                lT[:, rows(u, R), :] = swap(l0[rows(u, R)])
        loop(M, arrive)
        def product(c):
            pT[c] = dot(lT[c], rT[c], 1, 1).astype(jnp.bfloat16)
        loop(CB, product, 4)
        send_back(0, p)
        wait_back(0, p)
        def row(r, p=p):
            updated(0, pair, r, p, cur1)
        loop(R // G, row)
        project(1, cur1, p)
        if s > 0:
            send_left(1, p)
        send_right(1, p)
    send_left(1, q)

    def left_here(p):
        def one(u):
            pltpu.make_async_copy(lbuf.at[1, :, chans(u), lanes(p)], l1.at[rows(u, R), :, lanes(p)], l1r.at[u, p]).wait()
            lT[:, rows(u, R), lanes(p)] = swap(l1[rows(u, R), :, lanes(p)])
        loop(M, one)

    def right_here(p):
        def one(u):
            pltpu.make_async_copy(rbuf.at[1, :, chans(u), lanes(p)], r1.at[rows(u, R), :, lanes(p)], r1r.at[u, p]).wait()
            rT[:, rows(u, R), lanes(p)] = swap(r1[rows(u, R), :, lanes(p)])
        loop(M, one)

    def cross(d, p, k):
        return remote(xsend.at[d - 1, p, k * KB : (k + 1) * KB], xrecv.at[d - 1, p, k * KB : (k + 1) * KB],
                      xs.at[d - 1, p, k], xr.at[d - 1, p, k], lax.rem(q + d, Q) * M + m)

    for s in range(Q):
        p = lax.rem(q + s, Q)
        right_here(p)
        for d in range(1, Q):
            other = lax.rem(q + d, Q)
            if s == 0:
                left_here(other)
            for k in range(KS):
                def partial(i, d=d, p=p, other=other, k=k):
                    c = k * KB + i
                    xsend[d - 1, p, c] = dot(lT[c, :, lanes(other)], rT[c, :, lanes(p)], 0, 0).astype(jnp.bfloat16)
                loop(KB, partial, 4)
                cross(d, p, k).start()
    left_here(q)
    for p in range(Q):
        def mine(c, p=p):
            own[p, c] = dot(lT[c, :, lanes(q)], rT[c, :, lanes(p)], 0, 0)
        loop(CB, mine, 4)
    for s in range(Q):
        p = lax.rem(q + 1 + s, Q)
        for k in range(KS):
            for d in range(1, Q):
                cross(d, p, k).wait_recv()
            def total(i, p=p, k=k):
                c = k * KB + i
                v = own[p, c]
                for d in range(1, Q):
                    v = v + xrecv[d - 1, p, c].astype(jnp.float32)
                pT[c] = v.astype(jnp.bfloat16)
            loop(KB, total, 2)
        send_back(1, p)
        if s > 0:
            finish(lax.rem(q + s, Q))
    finish(lax.rem(q + Q, Q))
    def drain(i):
        u = lax.rem(m + 1 + i, M)
        for p in range(Q):
            left_copy(0, u, p, m).wait_send()
            left_copy(1, u, p, m).wait_send()
            right_copy(1, u, p, m).wait_send()
            for t in range(2):
                back_copy(t, u, p, m).wait_send()
    loop(M - 1, drain)
    def drain_right(i):
        d = lax.rem(me + 1 + i, N)
        for p in range(Q):
            right_copy(0, d, p, me).wait_send()
    loop(N - 1, drain_right)
    for p in range(Q):
        for d in range(1, Q):
            for k in range(KS):
                cross(d, p, k).wait_send()


def solution(mesh):
    N = mesh.shape["seq"] * mesh.shape["role"]
    roles = mesh.shape["role"]

    def local(pair, tri_gain, tri_proj, tri_gate, tri_mid_gain, tri_out, trans_gain, trans_up, trans_down):
        R, W, C = pair.shape
        inner = tri_out.shape[1]
        M = inner // CB
        Q = N // M
        bf, f32, vm, dma = jnp.bfloat16, jnp.float32, pltpu.VMEM, pltpu.SemaphoreType.DMA
        part = M * R
        assert part == LANES and Q * LANES == W
        X = max(Q - 1, 1)
        return pl.pallas_call(
            functools.partial(kernel, N, M, Q, R, roles),
            out_shape=jax.ShapeDtypeStruct((R, W, C), bf),
            in_specs=[pl.BlockSpec(memory_space=vm)] * 9,
            out_specs=pl.BlockSpec(memory_space=vm),
            scratch_shapes=[
                vm((2, R, inner, W), bf), vm((2, R, inner, W), bf),
                vm((R, W, C), bf), vm((R, W, C), f32),
                vm((part, CB, W), bf), vm((W, CB, W), bf),
                vm((part, CB, W), bf), vm((part, CB, W), bf),
                vm((CB, part, W), bf), vm((CB, part, W), bf), vm((CB, part, LANES), bf),
                vm((2, Q, M, R, CB, LANES), bf), vm((2, R, inner, W), bf),
                vm((X, Q, CB, part, LANES), bf), vm((X, Q, CB, part, LANES), bf),
                vm((Q, CB, part, LANES), f32),
                dma((M, Q)), dma((M, Q)), dma((N, Q)), dma((N, Q)),
                dma((M, Q)), dma((M, Q)), dma((M, Q)), dma((M, Q)),
                dma((2, M, Q)), dma((2, M, Q)), dma((X, Q, KS)), dma((X, Q, KS)),
            ],
            compiler_params=pltpu.CompilerParams(
                collective_id=0, has_side_effects=True, vmem_limit_bytes=66_000_000),
        )(pair, tri_gain, jnp.swapaxes(tri_proj, 1, 2), tri_gate, tri_mid_gain[:, :, None], tri_out,
          trans_gain[None, :], trans_up, trans_down)

    in_specs = (P(("groups", "seq", "role"), None, None), P(), P(), P(), P(), P(), P(), P(), P())
    out_specs = P(("groups", "seq", "role"), None, None)
    return jax.shard_map(local, mesh=mesh, in_specs=in_specs, out_specs=out_specs, check_vma=False)
```

```python
import functools

import jax
import jax.numpy as jnp
from jax import lax
from jax.experimental import pallas as pl
from jax.experimental.pallas import tpu as pltpu
from jax.sharding import PartitionSpec as P

epsilon = 1e-05
MESH = pl.DeviceIdType.MESH
LANES = 128
G = 4
KS = 2
CB = 16
KB = CB // KS


def sigmoid(v):
    return 0.5 * jnp.tanh(0.5 * v) + 0.5


def norm(v, gain, axis):
    average = jnp.mean(v, axis=axis, keepdims=True)
    centred = v - average
    spread = jnp.mean(centred * centred, axis=axis, keepdims=True)
    return (centred * lax.rsqrt(spread + epsilon) * gain).astype(jnp.bfloat16)


def dot(a, b, da, db):
    return lax.dot_general(a, b, (((da,), (db,)), ((), ())), preferred_element_type=jnp.float32)


def kernel(
    N, M, Q, R, roles,
    pair, gain, proj, gatew, midg, outw, tgain, up, down, out,
    lbuf, rbuf, cur1, gates, l0, r0, l1, r1, lT, rT, pT, psend, precv, xsend, xrecv, own,
    projT, midc,
    ls, lr, rs, rr, l1s, l1r, r1s, r1r, ps, pr, xs, xr,
):
    C = pair.shape[2]
    inner = outw.shape[1]
    hidden = down.shape[0]
    me = lax.axis_index("seq") * roles + lax.axis_index("role")
    q, m = lax.div(me, M), lax.rem(me, M)
    part = M * R

    def where(d):
        return {"seq": lax.div(d, roles), "role": lax.rem(d, roles)}

    def loop(count, body, unroll=1):
        def step(i, carry):
            body(i)
            return carry
        lax.fori_loop(0, count, step, 0, unroll=unroll)

    def lanes(p):
        return pl.ds(pl.multiple_of(p * LANES, LANES), LANES)

    def chans(u):
        return pl.ds(pl.multiple_of(u * CB, CB), CB)

    def rows(u, size):
        return pl.ds(pl.multiple_of(u * size, size), size)

    def remote(src, dst, ssem, rsem, d):
        return pltpu.make_async_remote_copy(
            src_ref=src, dst_ref=dst, send_sem=ssem, recv_sem=rsem,
            device_id=where(d), device_id_type=MESH)

    barrier = pltpu.get_barrier_semaphore()
    def greet(i):
        pl.semaphore_signal(barrier, inc=1, device_id=where(lax.rem(me + 1 + i, N)), device_id_type=MESH)
    loop(N - 1, greet)

    def tokens(cur, r, p):
        return cur[pl.ds(r * G, G), lanes(p), :].astype(jnp.float32).reshape(G * LANES, C)

    def turn(t):
        projT[t] = jnp.swapaxes(proj[t], 0, 1)
        midc[t] = jnp.swapaxes(jnp.broadcast_to(midg[t : t + 1, :], (LANES, inner)), 0, 1)

    def project(t, cur, p):
        def row(r):
            xn = norm(tokens(cur, r, p), gain[t : t + 1, :], 1)
            gates[pl.ds(r * G, G), lanes(p), :] = sigmoid(dot(xn, gatew[t], 1, 0)).reshape(G, LANES, C)
            for buf, at in ((lbuf, 0), (rbuf, 2 * inner)):
                pj = dot(projT[t, at : at + 2 * inner], xn, 1, 1)
                v = (pj[:inner] * sigmoid(pj[inner:])).astype(jnp.bfloat16)
                for g in range(G):
                    buf[t, r * G + g, :, lanes(p)] = v[:, g * LANES : (g + 1) * LANES]
        loop(R // G, row)

    def left_copy(t, u, p, src):
        dst, s, r_ = (l0, ls, lr) if t == 0 else (l1, l1s, l1r)
        return remote(lbuf.at[t, :, chans(u), lanes(p)], dst.at[rows(src, R), :, lanes(p)],
                      s.at[u, p], r_.at[src, p], q * M + u)

    def right_copy(t, d, p, src):
        if t == 0:
            return remote(rbuf.at[t, :, chans(lax.rem(d, M)), lanes(p)], r0.at[rows(src, R), :, lanes(p)],
                          rs.at[d, p], rr.at[src, p], d)
        return remote(rbuf.at[t, :, chans(d), lanes(p)], r1.at[rows(src, R), :, lanes(p)],
                      r1s.at[d, p], r1r.at[src, p], q * M + d)

    def self_copy(side, t, p):
        dl, sl = (l0, lr) if t == 0 else (l1, l1r)
        dr, sr, at = (r0, rr, me) if t == 0 else (r1, r1r, m)
        if side == 0:
            return pltpu.make_async_copy(lbuf.at[t, :, chans(m), lanes(p)], dl.at[rows(m, R), :, lanes(p)], sl.at[m, p])
        return pltpu.make_async_copy(rbuf.at[t, :, chans(m), lanes(p)], dr.at[rows(at, R), :, lanes(p)], sr.at[at, p])

    def send_left(t, p):
        self_copy(0, t, p).start()
        def near(i):
            left_copy(t, lax.rem(m + 1 + i, M), p, m).start()
        loop(M - 1, near)

    def send_right(t, p):
        self_copy(1, t, p).start()
        def near(i):
            u = lax.rem(m + 1 + i, M)
            right_copy(t, q * M + u if t == 0 else u, p, me if t == 0 else m).start()
        loop(M - 1, near)

    def send_far(p):
        def far(i):
            d = lax.rem(q + 1 + lax.div(i, M), Q) * M + lax.rem(m + i, M)
            right_copy(0, d, p, me).start()
        loop(N - M, far)

    def swap(x):
        return jnp.swapaxes(x, 0, 1)

    def back_copy(t, u, p, src):
        return remote(psend.at[t, p, u], precv.at[t, :, chans(src), lanes(p)],
                      ps.at[t, u, p], pr.at[t, src, p], q * M + u)

    def send_back(t, p):
        def one(u):
            psend[t, p, u] = swap(pT[:, rows(u, R), :])
        loop(M, one)
        pltpu.make_async_copy(psend.at[t, p, m], precv.at[t, :, chans(m), lanes(p)], pr.at[t, m, p]).start()
        def go(i):
            back_copy(t, lax.rem(m + 1 + i, M), p, m).start()
        loop(M - 1, go)

    def wait_back(t, p):
        def one(u):
            pltpu.make_async_copy(psend.at[t, p, u], precv.at[t, :, chans(u), lanes(p)], pr.at[t, u, p]).wait()
        loop(M, one)

    def updated(t, cur, r, p, to):
        for g in range(G):
            y = precv[t, r * G + g, :, lanes(p)].astype(jnp.float32)
            yn = norm(y, midc[t], 0)
            upd = dot(yn, outw[t], 0, 0)
            to[r * G + g, lanes(p), :] = (cur[r * G + g, lanes(p), :].astype(jnp.float32)
                                          + gates[r * G + g, lanes(p), :] * upd).astype(jnp.bfloat16)

    def finish(p):
        wait_back(1, p)
        def last(r):
            updated(1, cur1, r, p, cur1)
            cur = tokens(cur1, r, p)
            xn = norm(cur, tgain[...], 1)
            val = dot(xn, up[...], 1, 0)
            q0, q1 = val[:, :hidden], val[:, hidden:]
            h = (q0 * sigmoid(q0) * q1).astype(jnp.bfloat16)
            out[pl.ds(r * G, G), lanes(p), :] = (cur + dot(h, down[...], 1, 0)).astype(jnp.bfloat16).reshape(G, LANES, C)
        loop(R // G, last)

    turn(0)
    for s in range(Q):
        project(0, pair, s)
        if s == 0:
            pl.semaphore_wait(barrier, N - 1)
        send_left(0, s)
        send_right(0, s)
    for s in range(Q):
        send_far(s)
    turn(1)
    for s in range(Q):
        p = lax.rem(q + s, Q)
        def arrive(u, s=s, p=p):
            at = p * M + u
            for h in range(Q):
                pltpu.make_async_copy(rbuf.at[0, :, chans(u), lanes(h)], r0.at[rows(at, R), :, lanes(h)], rr.at[at, h]).wait()
                if s == 0:
                    pltpu.make_async_copy(lbuf.at[0, :, chans(u), lanes(h)], l0.at[rows(u, R), :, lanes(h)], lr.at[u, h]).wait()
            rT[:, rows(u, R), :] = swap(r0[rows(at, R)])
            if s == 0:
                lT[:, rows(u, R), :] = swap(l0[rows(u, R)])
        loop(M, arrive)
        def product(c):
            pT[c] = dot(lT[c], rT[c], 1, 1).astype(jnp.bfloat16)
        loop(CB, product, 4)
        send_back(0, p)
        wait_back(0, p)
        def row(r, p=p):
            updated(0, pair, r, p, cur1)
        loop(R // G, row)
        project(1, cur1, p)
        if s > 0:
            send_left(1, p)
        send_right(1, p)
    send_left(1, q)

    def left_here(p):
        def one(u):
            pltpu.make_async_copy(lbuf.at[1, :, chans(u), lanes(p)], l1.at[rows(u, R), :, lanes(p)], l1r.at[u, p]).wait()
            lT[:, rows(u, R), lanes(p)] = swap(l1[rows(u, R), :, lanes(p)])
        loop(M, one)

    def right_here(p):
        def one(u):
            pltpu.make_async_copy(rbuf.at[1, :, chans(u), lanes(p)], r1.at[rows(u, R), :, lanes(p)], r1r.at[u, p]).wait()
            rT[:, rows(u, R), lanes(p)] = swap(r1[rows(u, R), :, lanes(p)])
        loop(M, one)

    def cross(d, p, k):
        return remote(xsend.at[d - 1, p, k * KB : (k + 1) * KB], xrecv.at[d - 1, p, k * KB : (k + 1) * KB],
                      xs.at[d - 1, p, k], xr.at[d - 1, p, k], lax.rem(q + d, Q) * M + m)

    for s in range(Q):
        p = lax.rem(q + s, Q)
        right_here(p)
        for d in range(1, Q):
            other = lax.rem(q + d, Q)
            if s == 0:
                left_here(other)
            for k in range(KS):
                def partial(i, d=d, p=p, other=other, k=k):
                    c = k * KB + i
                    xsend[d - 1, p, c] = dot(lT[c, :, lanes(other)], rT[c, :, lanes(p)], 0, 0).astype(jnp.bfloat16)
                loop(KB, partial, 4)
                cross(d, p, k).start()
    left_here(q)
    for p in range(Q):
        def mine(c, p=p):
            own[p, c] = dot(lT[c, :, lanes(q)], rT[c, :, lanes(p)], 0, 0)
        loop(CB, mine, 4)
    for s in range(Q):
        p = lax.rem(q + 1 + s, Q)
        for k in range(KS):
            for d in range(1, Q):
                cross(d, p, k).wait_recv()
            def total(i, p=p, k=k):
                c = k * KB + i
                v = own[p, c]
                for d in range(1, Q):
                    v = v + xrecv[d - 1, p, c].astype(jnp.float32)
                pT[c] = v.astype(jnp.bfloat16)
            loop(KB, total, 2)
        send_back(1, p)
        if s > 0:
            finish(lax.rem(q + s, Q))
    finish(lax.rem(q + Q, Q))
    def drain(i):
        u = lax.rem(m + 1 + i, M)
        for p in range(Q):
            left_copy(0, u, p, m).wait_send()
            left_copy(1, u, p, m).wait_send()
            right_copy(1, u, p, m).wait_send()
            for t in range(2):
                back_copy(t, u, p, m).wait_send()
    loop(M - 1, drain)
    def drain_right(i):
        d = lax.rem(me + 1 + i, N)
        for p in range(Q):
            right_copy(0, d, p, me).wait_send()
    loop(N - 1, drain_right)
    for p in range(Q):
        for d in range(1, Q):
            for k in range(KS):
                cross(d, p, k).wait_send()


def solution(mesh):
    N = mesh.shape["seq"] * mesh.shape["role"]
    roles = mesh.shape["role"]

    def local(pair, tri_gain, tri_proj, tri_gate, tri_mid_gain, tri_out, trans_gain, trans_up, trans_down):
        R, W, C = pair.shape
        inner = tri_out.shape[1]
        M = inner // CB
        Q = N // M
        bf, f32, vm, dma = jnp.bfloat16, jnp.float32, pltpu.VMEM, pltpu.SemaphoreType.DMA
        part = M * R
        assert part == LANES and Q * LANES == W
        X = max(Q - 1, 1)
        return pl.pallas_call(
            functools.partial(kernel, N, M, Q, R, roles),
            out_shape=jax.ShapeDtypeStruct((R, W, C), bf),
            in_specs=[pl.BlockSpec(memory_space=vm)] * 9,
            out_specs=pl.BlockSpec(memory_space=vm),
            scratch_shapes=[
                vm((2, R, inner, W), bf), vm((2, R, inner, W), bf),
                vm((R, W, C), bf), vm((R, W, C), f32),
                vm((part, CB, W), bf), vm((W, CB, W), bf),
                vm((part, CB, W), bf), vm((part, CB, W), bf),
                vm((CB, part, W), bf), vm((CB, part, W), bf), vm((CB, part, LANES), bf),
                vm((2, Q, M, R, CB, LANES), bf), vm((2, R, inner, W), bf),
                vm((X, Q, CB, part, LANES), bf), vm((X, Q, CB, part, LANES), bf),
                vm((Q, CB, part, LANES), f32),
                vm((2, tri_proj.shape[2], C), bf), vm((2, inner, LANES), f32),
                dma((M, Q)), dma((M, Q)), dma((N, Q)), dma((N, Q)),
                dma((M, Q)), dma((M, Q)), dma((M, Q)), dma((M, Q)),
                dma((2, M, Q)), dma((2, M, Q)), dma((X, Q, KS)), dma((X, Q, KS)),
            ],
            compiler_params=pltpu.CompilerParams(
                collective_id=0, has_side_effects=True, vmem_limit_bytes=66_000_000),
        )(pair, tri_gain, tri_proj, tri_gate, tri_mid_gain, tri_out,
          trans_gain[None, :], trans_up, trans_down)

    in_specs = (P(("groups", "seq", "role"), None, None), P(), P(), P(), P(), P(), P(), P(), P())
    out_specs = P(("groups", "seq", "role"), None, None)
    return jax.shard_map(local, mesh=mesh, in_specs=in_specs, out_specs=out_specs, check_vma=False)
```
